768 devices in a mesh: dp: 16 (over y_hi, x), tensor: 48 (over z, y_lo, core).
Axes of the slice: x: 4, y: 8 (y_hi: 4, y_lo: 2; y = y_hi * 2 + y_lo), z: 12, core: 2. Of those that a mesh axis runs over, the one named last changes fastest.
Arguments:
- query_latent: bfloat16 [2, 6912, 1536], P(None, 'dp'), may hold values from -21 to 21
- key_latent: bfloat16 [2, 6912, 576], P(None, 'dp'), may hold values from -21 to 21
- partner: int32 [2, 48], replicated, may hold values from 0 to 47, as said below
- doc_length: int32 [2, 144], replicated, may hold values from 0 to 48, as said below
- up_query: bfloat16 [1536, 12288], P(None, 'tensor'), may hold values from -0.15625 to 0.15625
- up_rope: bfloat16 [1536, 6144], P(None, 'tensor'), may hold values from -0.15625 to 0.15625
- key_absorb: bfloat16 [12288, 512], P('tensor'), may hold values from -0.25 to 0.25
- value_expand: bfloat16 [512, 12288], P(None, 'tensor'), may hold values from -0.25 to 0.25
Outputs:
- head_out: bfloat16 [2, 6912, 12288], P(None, ('dp', 'tensor'))
The draws below stay inside these ranges and needn't reach their ends.
Inputs may be any that keep to these rules, and one draw needn't show every extreme that they name: In each microbatch partner pairs the groups: partner[m, partner[m, g]] = g and partner[m, g] != g; of each pair one group is full and the other holds 1 to 2 documents; group g lies on dp index g // 3, and in each microbatch at least one pair joins groups whose dp indices are 8 apart. `doc_length`: live slots of a group come first, each with 12 to 48 tokens, the rest have length 0; the last 1 slots of a full group are 48 tokens long.
All inputs are finite; a program needn't handle non-finite values.
Results may differ from the reference program's by a relative error of at most 0.012.
The reference program's roundings to bfloat16 on the way count: a program that leaves them out, or rounds other values in their place, can miss the bound.
Values may be sent and summed in bfloat16 or wider, within the bound.
A program may use at most 64 MiB of HBM per device.

```python
import jax
import jax.numpy as jnp
from jax import lax

Q_RANK = 1536
KV_RANK = 512
ROPE = 64
NOPE = 128
V_HEAD = 128
DOC = 48
SLOTS = 3
SEND = 1
MB = 2
GROUP_DEV = 3
GROUPS = 48
HEADS = 96


def latent_draw(key, array_shape):
    draw_key = jax.random.fold_in(key, 0)
    values = jax.random.normal(draw_key, array_shape, jnp.float32)
    return jnp.clip(values, -21.0, 21.0).astype(jnp.bfloat16)


def draw_query_latent(key, part):
    return latent_draw(jax.random.fold_in(key, 11), (MB, GROUPS * SLOTS * DOC, Q_RANK))


def draw_key_latent(key, part):
    return latent_draw(jax.random.fold_in(key, 12), (MB, GROUPS * SLOTS * DOC, KV_RANK + ROPE))


def move_front(order, target, place):
    found = jnp.argmax((order == target).astype(jnp.int32)).astype(jnp.int32)
    held = order[place]
    return order.at[found].set(held).at[place].set(target)


def matching(key):
    mates = []
    lengths = []
    half_groups = GROUPS // 2
    device_count = GROUPS // GROUP_DEV
    slot_index = jnp.arange(SLOTS).astype(jnp.int32)
    for micro_index in range(MB):
        micro_key = jax.random.fold_in(key, micro_index)
        order_key, count_key, length_key, cross_key, side_key = jax.random.split(micro_key, 5)
        picks = jax.random.randint(cross_key, (3,), 0, 1 << 20).astype(jnp.int32)
        first_device = picks[0] % device_count
        second_device = (first_device + device_count // 2) % device_count
        first_group = first_device * GROUP_DEV + picks[1] % GROUP_DEV
        second_group = second_device * GROUP_DEV + picks[2] % GROUP_DEV
        permuted = jax.random.permutation(order_key, GROUPS).astype(jnp.int32)
        permuted = move_front(permuted, first_group, 0)
        permuted = move_front(permuted, second_group, 1)
        even_ids = permuted[0::2]
        odd_ids = permuted[1::2]
        flip = jax.random.randint(side_key, (half_groups,), 0, 2).astype(jnp.int32) == 1
        heavy_ids = jnp.where(flip, even_ids, odd_ids)
        light_ids = jnp.where(flip, odd_ids, even_ids)
        mate_row = jnp.zeros((GROUPS,), jnp.int32).at[heavy_ids].set(light_ids).at[light_ids].set(heavy_ids)
        light_count = jax.random.randint(count_key, (half_groups,), 1, SLOTS - SEND + 1).astype(jnp.int32)
        doc_count = jnp.zeros((GROUPS,), jnp.int32).at[heavy_ids].set(SLOTS).at[light_ids].set(light_count)
        length = jax.random.randint(length_key, (GROUPS, SLOTS), DOC // 4, DOC + 1).astype(jnp.int32)
        is_full = (doc_count == SLOTS)[:, None] & (slot_index >= SLOTS - SEND)[None, :]
        length = jnp.where(is_full, DOC, length)
        length = jnp.where(slot_index[None, :] < doc_count[:, None], length, 0)
        mates.append(mate_row)
        lengths.append(length.reshape(GROUPS * SLOTS))
    return (jnp.stack(mates), jnp.stack(lengths))


def draw_partner(key, part):
    return matching(jax.random.fold_in(key, 7))[0]


def draw_doc_length(key, part):
    return matching(jax.random.fold_in(key, 7))[1]


def levels(key, extent, pieces, least, high):
    level = 1.0
    for axis_at, blocks in pieces:
        steps = jax.random.uniform(jax.random.fold_in(jax.random.fold_in(key, 6), axis_at), (blocks,), jnp.float32, least / len(pieces), high / len(pieces))
        level = level * jnp.repeat(jnp.exp(steps), extent[axis_at] // blocks).reshape((-1,) + (1,) * (len(extent) - 1 - axis_at))
    return level


def bell_draw(rng, dims, spread, most, cuts=(), kind=jnp.bfloat16):
    level = levels(rng, dims, cuts, -0.22, 0.18) if cuts else 1.0
    values = jax.random.normal(rng, dims, jnp.float32) * spread * level
    return jnp.minimum(jnp.maximum(values, -most), most).astype(kind)


def setup_inputs(seed: int = 0) -> dict:
    key_list = jax.random.split(jax.random.key(seed), 9)
    query_latent = draw_query_latent(jax.random.fold_in(key_list[8], 71), 0)
    key_latent = draw_key_latent(jax.random.fold_in(key_list[8], 71), 0)
    partner = draw_partner(jax.random.fold_in(key_list[8], 71), 0)
    doc_length = draw_doc_length(jax.random.fold_in(key_list[8], 71), 0)
    up_query = bell_draw(key_list[4], (Q_RANK, HEADS * NOPE), Q_RANK ** -0.5, 0.15625, ((1, 48),))
    up_rope = bell_draw(key_list[5], (Q_RANK, HEADS * ROPE), Q_RANK ** -0.5, 0.15625, ((1, 48),))
    key_absorb = bell_draw(key_list[6], (HEADS * NOPE, KV_RANK), KV_RANK ** -0.5, 0.25, ((0, 48),))
    value_expand = bell_draw(key_list[7], (KV_RANK, HEADS * V_HEAD), KV_RANK ** -0.5, 0.25, ((1, 48),))
    return dict(query_latent=query_latent, key_latent=key_latent, partner=partner, doc_length=doc_length, up_query=up_query, up_rope=up_rope, key_absorb=key_absorb, value_expand=value_expand)


def rotation(row_count, half_width):
    position = (jnp.arange(row_count).astype(jnp.int32) % DOC).astype(jnp.float32)
    inverse_freq = 10000.0 ** (-jnp.arange(half_width).astype(jnp.float32) / half_width)
    angles = position[:, None] * inverse_freq[None, :]
    return jnp.cos(angles), jnp.sin(angles)


def rotate(values, cosine, sine_part):
    half_width = values.shape[-1] // 2
    lower_half = values[..., :half_width]
    upper_half = values[..., half_width:]
    return jnp.concatenate([lower_half * cosine - upper_half * sine_part, upper_half * cosine + lower_half * sine_part], -1)


def attend(query_rows, key_rows, lengths, up_query, up_rope, key_absorb, value_expand):
    batches, row_count, _ = query_rows.shape
    head_count = key_absorb.shape[0] // NOPE
    blocks = row_count // DOC
    flat_rows = query_rows.reshape(batches * row_count, Q_RANK)
    query_nope = jnp.dot(flat_rows, up_query, preferred_element_type=jnp.float32).astype(jnp.bfloat16)
    query_nope = query_nope.reshape(batches * row_count, head_count, NOPE)
    absorb = key_absorb.reshape(head_count, NOPE, KV_RANK)
    absorbed = jnp.einsum("rhd,hdc->rhc", query_nope.astype(jnp.float32), absorb.astype(jnp.float32)).astype(jnp.bfloat16)
    cosine, sine_part = rotation(row_count, ROPE // 2)
    query_rope = jnp.dot(flat_rows, up_rope, preferred_element_type=jnp.float32).reshape(batches, row_count, head_count, ROPE)
    query_rope = rotate(query_rope, cosine[:, None, :], sine_part[:, None, :]).astype(jnp.bfloat16)
    latent = key_rows[..., :KV_RANK]
    key_rope = rotate(key_rows[..., KV_RANK:].astype(jnp.float32), cosine, sine_part).astype(jnp.bfloat16)
    queries = jnp.concatenate([absorbed.reshape(batches, row_count, head_count, KV_RANK), query_rope], -1)
    queries = queries.reshape(batches, blocks, DOC, head_count, KV_RANK + ROPE)
    key_full = jnp.concatenate([latent, key_rope], -1).reshape(batches, blocks, DOC, KV_RANK + ROPE)
    scores = jnp.einsum("bnqhc,bnkc->bnhqk", queries.astype(jnp.float32), key_full.astype(jnp.float32))
    scores = scores * (NOPE + ROPE) ** -0.5
    query_pos = jnp.arange(DOC).astype(jnp.int32)[:, None]
    key_pos = jnp.arange(DOC).astype(jnp.int32)[None, :]
    live_len = lengths.reshape(batches, blocks)[:, :, None, None, None]
    allowed = (key_pos <= query_pos) & ((key_pos < live_len) | (key_pos == query_pos))
    scores = jnp.where(allowed, scores, -jnp.inf)
    row_max = jnp.max(scores, -1, keepdims=True)
    weights = jnp.exp(scores - row_max)
    probability = (weights / jnp.sum(weights, -1, keepdims=True)).astype(jnp.bfloat16)
    latent_blocks = latent.reshape(batches, blocks, DOC, KV_RANK)
    mixed_latent = jnp.einsum("bnhqk,bnkc->bnqhc", probability.astype(jnp.float32), latent_blocks.astype(jnp.float32)).astype(jnp.bfloat16)
    expand = value_expand.reshape(KV_RANK, head_count, V_HEAD)
    result = jnp.einsum("bnqhc,chv->bnqhv", mixed_latent.astype(jnp.float32), expand.astype(jnp.float32))
    live_rows = jnp.arange(DOC).astype(jnp.int32)[None, None, :] < lengths.reshape(batches, blocks)[:, :, None]
    result = jnp.where(live_rows[:, :, :, None, None], result, 0.0).astype(jnp.bfloat16)
    return result.reshape(batches, row_count, head_count * V_HEAD)


def reference(query_latent, key_latent, partner, doc_length, up_query, up_rope, key_absorb, value_expand):
    group_rows = SLOTS * DOC
    slot_sent = jnp.arange(SLOTS).astype(jnp.int32) >= SLOTS - SEND
    row_sent = (jnp.arange(group_rows).astype(jnp.int32) // DOC >= SLOTS - SEND)[:, None]
    outputs = []
    for micro_index in range(MB):
        length_table = doc_length[micro_index].reshape(GROUPS, SLOTS)
        counts = jnp.sum((length_table > 0).astype(jnp.int32), 1)
        query_micro = query_latent[micro_index]
        key_micro = key_latent[micro_index]
        mates = partner[micro_index]

        def one_group(my_group):
            mate_index = mates[my_group]
            is_heavy = counts[my_group] == SLOTS
            own_start = (my_group * group_rows).astype(jnp.int32)
            mate_start = (mate_index * group_rows).astype(jnp.int32)
            own_query = lax.dynamic_slice_in_dim(query_micro, own_start, group_rows, 0)
            own_key = lax.dynamic_slice_in_dim(key_micro, own_start, group_rows, 0)
            mate_query = lax.dynamic_slice_in_dim(query_micro, mate_start, group_rows, 0)
            mate_key = lax.dynamic_slice_in_dim(key_micro, mate_start, group_rows, 0)
            take_mate = row_sent & jnp.logical_not(is_heavy)
            source_q = jnp.where(take_mate, mate_query, own_query)
            source_kv = jnp.where(take_mate, mate_key, own_key)
            mate_lengths = jnp.where(is_heavy, 0, length_table[mate_index])
            lengths = jnp.where(slot_sent, mate_lengths, length_table[my_group])
            result = attend(source_q[None], source_kv[None], lengths[None], up_query, up_rope, key_absorb, value_expand)
            return result[0]

        result = lax.map(one_group, jnp.arange(GROUPS).astype(jnp.int32))
        outputs.append(result.reshape(GROUPS * group_rows, HEADS * V_HEAD))
    return jnp.stack(outputs)
```

```python
import functools

import jax
import jax.numpy as jnp
import numpy as np
from jax import lax
from jax.experimental import pallas as pl
from jax.experimental.pallas import tpu as pltpu
from jax.sharding import PartitionSpec as P

Q_RANK = 1536
KV_RANK = 512
ROPE = 64
NOPE = 128
V_HEAD = 128
DOC = 48
SLOTS = 3
GROUP_DEV = 3
ROWS = SLOTS * DOC
MB = 2
MESH = pl.DeviceIdType.MESH
X_DEV = 4
Y_DEV = 4
RANKS = 48
OWN_ROWS = 9
CUT = 10
TAIL = CUT * OWN_ROWS


def rope_tables():
    freq = 10000.0 ** (-np.arange(32, dtype=np.float32) / np.float32(32))
    angles = np.arange(DOC, dtype=np.float32)[:, None] * freq.astype(np.float32)[None, :]
    cosine = np.cos(angles.astype(np.float64)).astype(np.float32)
    sine = np.sin(angles.astype(np.float64)).astype(np.float32)
    cos_row = np.concatenate([cosine] * 4, 1)
    sin_row = np.concatenate([-sine, sine, -sine, sine], 1)
    return np.stack([cos_row, sin_row])


def dot(a, b, dims=((1,), (0,))):
    return lax.dot_general(a, b, (dims, ((), ())), preferred_element_type=jnp.float32)


def rotate_pairs(values, cosine, sine):
    lane = lax.broadcasted_iota(jnp.int32, values.shape, 1)
    swapped = jnp.where(
        lane % 64 < 32, pltpu.roll(values, 96, 1), pltpu.roll(values, 32, 1)
    )
    return values * cosine + swapped * sine


def compute_kernel(len_ref, q_ref, k_ref, uq_ref, ur_ref, ab_ref, ve_ref, tab_ref, o_ref, mix_ref):
    my_dp = lax.axis_index("dp")
    scale = (NOPE + ROPE) ** -0.5
    row_pos = lax.broadcasted_iota(jnp.int32, (2 * DOC, DOC), 0) % DOC
    key_pos = lax.broadcasted_iota(jnp.int32, (2 * DOC, DOC), 1)
    out_pos = lax.broadcasted_iota(jnp.int32, (DOC, 2 * V_HEAD), 0)
    lane = lax.broadcasted_iota(jnp.int32, (DOC, 128), 1)

    def group(b, carry):
        m = b // GROUP_DEV
        j = b % GROUP_DEV
        rows = pl.ds(pl.multiple_of(j * ROWS, ROWS), ROWS)
        x = q_ref[m, rows, :]
        nope = dot(x, uq_ref[...]).astype(jnp.bfloat16)
        rope = dot(x, ur_ref[...])
        absorbed = [
            dot(nope[:, h * NOPE : (h + 1) * NOPE], ab_ref[h * NOPE : (h + 1) * NOPE, :]).astype(
                jnp.bfloat16
            )
            for h in range(2)
        ]
        for s in range(SLOTS):
            lo, hi = s * DOC, (s + 1) * DOC
            here = pl.ds(pl.multiple_of(j * ROWS + s * DOC, DOC), DOC)
            latent = k_ref[m, here, 0:KV_RANK]
            kr = k_ref[m, here, KV_RANK : KV_RANK + ROPE].astype(jnp.float32)
            kr = jnp.concatenate([kr, kr], 1)
            kr = rotate_pairs(kr, tab_ref[0], tab_ref[1]).astype(jnp.bfloat16)
            qr = rotate_pairs(rope[lo:hi], tab_ref[0], tab_ref[1])
            qr = jnp.concatenate(
                [jnp.where(lane < 64, qr, 0.0), jnp.where(lane < 64, 0.0, qr)], 0
            ).astype(jnp.bfloat16)
            qa = jnp.concatenate([absorbed[0][lo:hi], absorbed[1][lo:hi]], 0)
            scores = dot(qa, latent, ((1,), (1,))) + dot(qr, kr, ((1,), (1,)))
            length = len_ref[m, (my_dp * GROUP_DEV + j) * SLOTS + s]
            allowed = (key_pos <= row_pos) & ((key_pos < length) | (key_pos == row_pos))
            scores = jnp.where(allowed, scores * scale, -jnp.inf)
            weights = jnp.exp(scores - jnp.max(scores, 1, keepdims=True))
            prob = (weights / jnp.sum(weights, 1, keepdims=True)).astype(jnp.bfloat16)
            mixed = dot(prob, latent).astype(jnp.bfloat16)
            mix_ref[0, lo:hi, :] = mixed[:DOC]
            mix_ref[1, lo:hi, :] = mixed[DOC:]
        for h in range(2):
            res = dot(mix_ref[h], ve_ref[:, h * V_HEAD : (h + 1) * V_HEAD])
            for s in range(SLOTS):
                here = pl.ds(pl.multiple_of(j * ROWS + s * DOC, DOC), DOC)
                length = len_ref[m, (my_dp * GROUP_DEV + j) * SLOTS + s]
                part = jnp.where(out_pos[:, :V_HEAD] < length, res[s * DOC : (s + 1) * DOC], 0.0)
                o_ref[m, here, h * V_HEAD : (h + 1) * V_HEAD] = part.astype(jnp.bfloat16)
        return carry

    lax.fori_loop(0, MB * GROUP_DEV, group, 0)


def compute(doc_length, query, key, up_query, up_rope, key_absorb, value_expand):
    vm = pl.BlockSpec(memory_space=pltpu.VMEM)
    return pl.pallas_call(
        compute_kernel,
        out_shape=jax.ShapeDtypeStruct((MB, GROUP_DEV * ROWS, 2 * V_HEAD), jnp.bfloat16),
        in_specs=[pl.BlockSpec(memory_space=pltpu.SMEM)] + [vm] * 7,
        out_specs=vm,
        scratch_shapes=[pltpu.VMEM((2, ROWS, KV_RANK), jnp.bfloat16)],
        name="attend",
    )(doc_length, query, key, up_query, up_rope, key_absorb, value_expand, jnp.asarray(rope_tables()))


def comm_kernel(
    partner_ref,
    len_ref,
    in_ref,
    out_ref,
    recv1,
    snd2,
    recv2,
    merged,
    local_sem,
    y_send,
    y_recv,
    x_send,
    x_recv,
    t_send,
    t_recv,
):
    me_dp = lax.axis_index("dp")
    me_t = lax.axis_index("tensor")
    me_x = me_dp % X_DEV
    me_y = me_dp // X_DEV

    def y_peer(step):
        return lax.rem(me_y + step, Y_DEV) * X_DEV + me_x

    def x_peer(step):
        return me_y * X_DEV + lax.rem(me_x + step, X_DEV)

    barrier = pltpu.get_barrier_semaphore()
    for step in range(1, Y_DEV):
        pl.semaphore_signal(
            barrier, inc=1, device_id={"dp": y_peer(step), "tensor": me_t}, device_id_type=MESH
        )
    for step in range(1, X_DEV):
        pl.semaphore_signal(
            barrier, inc=1, device_id={"dp": x_peer(step), "tensor": me_t}, device_id_type=MESH
        )

    def greet(step, carry):
        pl.semaphore_signal(
            barrier,
            inc=1,
            device_id={"dp": me_dp, "tensor": lax.rem(me_t + step, RANKS)},
            device_id_type=MESH,
        )
        return carry

    lax.fori_loop(1, RANKS, greet, 0)
    tail_copy = pltpu.make_async_copy(
        in_ref.at[:, pl.ds(TAIL, SLOTS * DOC - DOC - TAIL)],
        merged.at[:, pl.ds(0, SLOTS * DOC - DOC - TAIL)],
        local_sem.at[0],
    )
    tail_copy.start()
    docs = in_ref.at[:, pl.ds((SLOTS - 1) * DOC, DOC)]
    own_copy = pltpu.make_async_copy(docs, recv1.at[me_y], local_sem.at[1])
    own_copy.start()
    pl.semaphore_wait(barrier, RANKS - 1 + X_DEV - 1 + Y_DEV - 1)

    def y_copy(step):
        return pltpu.make_async_remote_copy(
            src_ref=docs,
            dst_ref=recv1.at[me_y],
            send_sem=y_send.at[step - 1],
            recv_sem=y_recv.at[step - 1],
            device_id={"dp": y_peer(step), "tensor": me_t},
            device_id_type=MESH,
        )

    for step in (2, 1, 3):
        y_copy(step).start()

    def t_copy(rank, source):
        return pltpu.make_async_remote_copy(
            src_ref=source,
            dst_ref=out_ref.at[:, :, pl.ds(pl.multiple_of(me_t * 256, 256), 256)],
            send_sem=t_send.at[rank],
            recv_sem=t_recv.at[me_t],
            device_id={"dp": me_dp, "tensor": rank},
            device_id_type=MESH,
        )

    def self_copy(source):
        return pltpu.make_async_copy(
            source,
            out_ref.at[:, :, pl.ds(pl.multiple_of(me_t * 256, 256), 256)],
            local_sem.at[2],
        )

    def first_source(rank):
        return in_ref.at[rank // 16, pl.ds((rank % 16) * OWN_ROWS, OWN_ROWS)]

    def second_source(rank):
        return merged.at[rank // 16, pl.ds((rank % 16 - CUT) * OWN_ROWS, OWN_ROWS)]

    def send_first(step, carry):
        rank = lax.rem(me_t + step, RANKS)

        @pl.when(rank % 16 < CUT)
        def _():
            t_copy(rank, first_source(rank)).start()

        return carry

    lax.fori_loop(1, RANKS, send_first, 0)

    @pl.when(me_t % 16 < CUT)
    def _():
        self_copy(first_source(me_t)).start()

    own_copy.wait()
    tail_copy.wait()
    for step in range(1, Y_DEV):
        y_copy(step).wait_recv()

    micro = lax.broadcasted_iota(jnp.int32, (DOC, MB, 2 * V_HEAD), 1)

    def wanted(x_at, j, m):
        return partner_ref[m, (me_y * X_DEV + x_at) * GROUP_DEV + j]

    for step in range(X_DEV):
        x_at = lax.rem(me_x + step, X_DEV)
        for j in range(GROUP_DEV):
            first = wanted(x_at, j, 0)
            second = wanted(x_at, j, 1)
            a = recv1[first // (X_DEV * GROUP_DEV), first % GROUP_DEV]
            b = recv1[second // (X_DEV * GROUP_DEV), second % GROUP_DEV]
            picked = jnp.where(micro == 0, a, b)
            if step == 0:
                recv2[me_x, j] = picked
            else:
                snd2[step - 1, j] = picked

    def x_copy(step):
        return pltpu.make_async_remote_copy(
            src_ref=snd2.at[step - 1],
            dst_ref=recv2.at[me_x],
            send_sem=x_send.at[step - 1],
            recv_sem=x_recv.at[step - 1],
            device_id={"dp": x_peer(step), "tensor": me_t},
            device_id_type=MESH,
        )

    for step in (2, 1, 3):
        x_copy(step).start()
    for step in range(1, X_DEV):
        x_copy(step).wait_recv()

    for j in range(GROUP_DEV):
        picks = []
        for m in range(MB):
            group = me_dp * GROUP_DEV + j
            source_x = (partner_ref[m, group] // GROUP_DEV) % X_DEV
            live = jnp.int32(0)
            for s in range(SLOTS):
                live += (len_ref[m, group * SLOTS + s] > 0).astype(jnp.int32)
            value = recv2[source_x, j]
            picks.append(jnp.where(live < SLOTS, value, jnp.zeros_like(value)))
        merged[j, pl.ds(SLOTS * DOC - DOC - TAIL, DOC)] = jnp.where(micro == 0, picks[0], picks[1])

    def send_second(step, carry):
        rank = lax.rem(me_t + step, RANKS)

        @pl.when(rank % 16 >= CUT)
        def _():
            t_copy(rank, second_source(rank)).start()

        return carry

    lax.fori_loop(1, RANKS, send_second, 0)

    @pl.when(me_t % 16 >= CUT)
    def _():
        self_copy(second_source(me_t)).start()

    def finish(step, carry):
        source = lax.rem(me_t + step, RANKS)
        pltpu.make_async_remote_copy(
            src_ref=merged.at[0, pl.ds(0, OWN_ROWS)],
            dst_ref=out_ref.at[:, :, pl.ds(pl.multiple_of(source * 256, 256), 256)],
            send_sem=t_send.at[source],
            recv_sem=t_recv.at[source],
            device_id={"dp": me_dp, "tensor": source},
            device_id_type=MESH,
        ).wait()
        return carry

    lax.fori_loop(1, RANKS, finish, 0)
    self_copy(merged.at[0, pl.ds(0, OWN_ROWS)]).wait()
    for step in range(1, Y_DEV):
        y_copy(step).wait_send()
    for step in range(1, X_DEV):
        x_copy(step).wait_send()


def exchange(partner, doc_length, produced):
    docs = (GROUP_DEV, DOC, MB, 2 * V_HEAD)
    smem = pl.BlockSpec(memory_space=pltpu.SMEM)
    vm = pl.BlockSpec(memory_space=pltpu.VMEM)
    return pl.pallas_call(
        comm_kernel,
        out_shape=jax.ShapeDtypeStruct((OWN_ROWS, MB, RANKS * 2 * V_HEAD), jnp.bfloat16),
        in_specs=[smem, smem, vm],
        out_specs=vm,
        scratch_shapes=[
            pltpu.VMEM((Y_DEV,) + docs, jnp.bfloat16),
            pltpu.VMEM((X_DEV - 1,) + docs, jnp.bfloat16),
            pltpu.VMEM((X_DEV,) + docs, jnp.bfloat16),
            pltpu.VMEM((GROUP_DEV, ROWS - TAIL, MB, 2 * V_HEAD), jnp.bfloat16),
            pltpu.SemaphoreType.DMA((3,)),
            pltpu.SemaphoreType.DMA((Y_DEV - 1,)),
            pltpu.SemaphoreType.DMA((Y_DEV - 1,)),
            pltpu.SemaphoreType.DMA((X_DEV - 1,)),
            pltpu.SemaphoreType.DMA((X_DEV - 1,)),
            pltpu.SemaphoreType.DMA((RANKS,)),
            pltpu.SemaphoreType.DMA((RANKS,)),
        ],
        compiler_params=pltpu.CompilerParams(collective_id=0, has_side_effects=True),
        name="exchange",
    )(partner, doc_length, produced)


def body(
    query_latent, key_latent, partner, doc_length, up_query, up_rope, key_absorb, value_expand
):
    produced = compute(
        doc_length, query_latent, key_latent, up_query, up_rope, key_absorb, value_expand
    )
    produced = produced.reshape(MB, GROUP_DEV, ROWS, 2 * V_HEAD).transpose(1, 2, 0, 3)
    result = exchange(partner, doc_length, produced)
    return result.transpose(1, 0, 2)


def solution(mesh):
    in_specs = (
        P(None, "dp", None),
        P(None, "dp", None),
        P(),
        P(),
        P(None, "tensor"),
        P(None, "tensor"),
        P("tensor", None),
        P(None, "tensor"),
    )
    out_specs = P(None, ("dp", "tensor"), None)
    return jax.shard_map(body, mesh=mesh, in_specs=in_specs, out_specs=out_specs, check_vma=False)
```

```python
import jax
import jax.numpy as jnp
import numpy as np
from jax import lax
from jax.experimental import pallas as pl
from jax.experimental.pallas import tpu as pltpu
from jax.sharding import PartitionSpec as P

Q_RANK = 1536
KV_RANK = 512
ROPE = 64
NOPE = 128
V_HEAD = 128
DOC = 48
SLOTS = 3
GROUP_DEV = 3
ROWS = SLOTS * DOC
MB = 2
PAIR = MB * DOC
UNITS = GROUP_DEV * SLOTS
BLOCK = 3
MESH = pl.DeviceIdType.MESH
X_DEV = 4
Y_DEV = 4
RANKS = 48
OWN_ROWS = 9
SHARE = ROWS // OWN_ROWS
CUT = 10
TAIL = CUT * OWN_ROWS
HALF = (SLOTS - 1) * DOC - TAIL
CHUNKS = 3
CHUNK = PAIR // CHUNKS
BF16 = jnp.bfloat16


def rope_tables():
    freq = 10000.0 ** (-np.arange(32, dtype=np.float32) / np.float32(32))
    angles = np.arange(DOC, dtype=np.float32)[:, None] * freq.astype(np.float32)[None, :]
    cosine = np.cos(angles.astype(np.float64)).astype(np.float32)
    sine = np.sin(angles.astype(np.float64)).astype(np.float32)
    cos_row = np.concatenate([cosine] * 4, 1)
    sin_row = np.concatenate([-sine, sine, -sine, sine], 1)
    return np.stack([np.concatenate([t] * MB, 0) for t in (cos_row, sin_row)])


def dot(a, b, dims=((1,), (0,))):
    return lax.dot_general(a, b, (dims, ((), ())), preferred_element_type=jnp.float32)


def rotate_pairs(values, cosine, sine):
    lane = lax.broadcasted_iota(jnp.int32, values.shape, 1)
    swapped = jnp.where(
        lane % 64 < 32, pltpu.roll(values, 96, 1), pltpu.roll(values, 32, 1)
    )
    return values * cosine + swapped * sine


def unit_place(unit):
    if unit < GROUP_DEV:
        return unit, SLOTS - 1
    return (unit - GROUP_DEV) // (SLOTS - 1), (unit - GROUP_DEV) % (SLOTS - 1)


def kernel(
    partner_ref,
    len_ref,
    q_ref,
    k_ref,
    uq_ref,
    ur_ref,
    ab_ref,
    ve_ref,
    tab_ref,
    out_ref,
    xbuf,
    kbuf,
    uq,
    ur,
    ab,
    ve,
    tab,
    front,
    docs,
    recv1_a,
    recv1_b,
    recv1_c,
    snd2,
    recv2_a,
    recv2_b,
    recv2_c,
    final,
    load_sem,
    local_sem,
    own_sem,
    y_send,
    y_recv,
    x_send,
    x_recv,
    t_send,
    t_recv,
    h_send,
    h_recv,
):
    recv1 = (recv1_a, recv1_b, recv1_c)
    recv2 = (recv2_a, recv2_b, recv2_c)
    me_dp = lax.axis_index("dp")
    me_t = lax.axis_index("tensor")
    me_x = me_dp % X_DEV
    me_y = me_dp // X_DEV

    def y_peer(step):
        return lax.rem(me_y + step, Y_DEV) * X_DEV + me_x

    def x_peer(step):
        return me_y * X_DEV + lax.rem(me_x + step, X_DEV)

    def load_units(units, half):
        for unit in units:
            j, s = unit_place(unit)
            rows = pl.ds(j * ROWS + s * DOC, DOC)
            for m in range(MB):
                at = pl.ds(unit * PAIR + m * DOC, DOC)
                pltpu.make_async_copy(q_ref.at[m, rows], xbuf.at[at], load_sem.at[half]).start()
                pltpu.make_async_copy(k_ref.at[m, rows], kbuf.at[at], load_sem.at[2 + half]).start()

    def wait_units(first, count, half):
        at = pl.ds(first * PAIR, count * PAIR)
        pltpu.make_async_copy(xbuf.at[at], xbuf.at[at], load_sem.at[half]).wait()
        pltpu.make_async_copy(kbuf.at[at], kbuf.at[at], load_sem.at[2 + half]).wait()

    weights = ((uq_ref, uq), (ur_ref, ur), (tab_ref, tab), (ab_ref, ab), (ve_ref, ve))

    def weight_copy(n):
        return pltpu.make_async_copy(weights[n][0], weights[n][1], load_sem.at[4 + n])

    weight_copy(0).start()
    load_units(range(BLOCK), 0)
    for n in range(1, 5):
        weight_copy(n).start()
    load_units(range(BLOCK, UNITS), 1)

    barrier = pltpu.get_barrier_semaphore()

    def greet(step, carry):
        pl.semaphore_signal(
            barrier,
            inc=1,
            device_id={"dp": me_dp, "tensor": lax.rem(me_t + step, RANKS)},
            device_id_type=MESH,
        )
        return carry

    lax.fori_loop(1, RANKS, greet, 0)
    for step in range(1, Y_DEV):
        pl.semaphore_signal(
            barrier, inc=1, device_id={"dp": y_peer(step), "tensor": me_t}, device_id_type=MESH
        )
    for step in range(1, X_DEV):
        pl.semaphore_signal(
            barrier, inc=1, device_id={"dp": x_peer(step), "tensor": me_t}, device_id_type=MESH
        )

    scale = (NOPE + ROPE) ** -0.5
    perm_row = lax.broadcasted_iota(jnp.int32, (PAIR, PAIR), 0)
    perm_col = lax.broadcasted_iota(jnp.int32, (PAIR, PAIR), 1)
    perm = (perm_col == (perm_row % MB) * DOC + perm_row // MB).astype(jnp.float32).astype(BF16)
    row_at = lax.broadcasted_iota(jnp.int32, (2 * PAIR, PAIR), 0) % PAIR
    row_micro = row_at % MB
    row_pos = row_at // MB
    key_at = lax.broadcasted_iota(jnp.int32, (2 * PAIR, PAIR), 1)
    key_pos = key_at % DOC
    causal = (key_at // DOC == row_micro) & (key_pos <= row_pos)
    diagonal = key_pos == row_pos
    out_at = lax.broadcasted_iota(jnp.int32, (PAIR, V_HEAD), 0)
    lane = lax.broadcasted_iota(jnp.int32, (PAIR, 128), 1)
    head_lane = [(lane // ROPE == h).astype(jnp.float32).astype(BF16) for h in range(2)]

    def compute(block):
        rows = slice(block * BLOCK * PAIR, (block + 1) * BLOCK * PAIR)
        x = xbuf[rows, :]
        nope = dot(x, uq[...]).astype(BF16)
        rope = dot(x, ur[...])
        mixed_all = [[], []]
        ordered = []
        for i in range(BLOCK):
            at = slice(i * PAIR, (i + 1) * PAIR)
            turned = rotate_pairs(rope[at], tab[0], tab[1]).astype(BF16)
            both = jnp.concatenate([nope[at], turned], 1)
            ordered.append(dot(perm, both).astype(BF16))
        ordered = jnp.concatenate(ordered, 0)
        absorbed = [
            dot(ordered[:, h * NOPE : (h + 1) * NOPE], ab[h * NOPE : (h + 1) * NOPE, :]).astype(BF16)
            for h in range(2)
        ]
        lengths = []
        for i in range(BLOCK):
            unit = block * BLOCK + i
            j, s = unit_place(unit)
            at = slice(i * PAIR, (i + 1) * PAIR)
            here = slice(unit * PAIR, (unit + 1) * PAIR)
            latent = kbuf[here, 0:KV_RANK]
            kr = kbuf[here, KV_RANK : KV_RANK + ROPE].astype(jnp.float32)
            kr = rotate_pairs(jnp.concatenate([kr, kr], 1), tab[0], tab[1]).astype(BF16)
            keys = jnp.concatenate([latent, kr], 1)
            qr = ordered[at, 2 * NOPE :]
            queries = jnp.concatenate(
                [
                    jnp.concatenate([absorbed[h][at], qr * head_lane[h]], 1)
                    for h in range(2)
                ],
                0,
            )
            scores = dot(queries, keys, ((1,), (1,)))
            slot = (me_dp * GROUP_DEV + j) * SLOTS + s
            pair_len = [len_ref[m, slot] for m in range(MB)]
            lengths.append(pair_len)
            live = jnp.where(row_micro == 0, pair_len[0], pair_len[1])
            allowed = causal & ((key_pos < live) | diagonal)
            scores = jnp.where(allowed, scores * scale, -jnp.inf)
            weight = jnp.exp(scores - jnp.max(scores, 1, keepdims=True))
            prob = (weight / jnp.sum(weight, 1, keepdims=True)).astype(BF16)
            mixed = dot(prob, latent).astype(BF16)
            for h in range(2):
                mixed_all[h].append(mixed[h * PAIR : (h + 1) * PAIR])
        for h in range(2):
            res = dot(jnp.concatenate(mixed_all[h], 0), ve[:, h * V_HEAD : (h + 1) * V_HEAD])
            for i in range(BLOCK):
                j, s = unit_place(block * BLOCK + i)
                live = jnp.where(out_at % MB == 0, lengths[i][0], lengths[i][1])
                part = jnp.where(out_at // MB < live, res[i * PAIR : (i + 1) * PAIR], 0.0)
                part = part.astype(BF16)
                if block == 0:
                    docs[j, h] = part
                else:
                    front.at[j, h].reshape((SLOTS - 1) * PAIR, V_HEAD)[
                        s * PAIR : (s + 1) * PAIR, :
                    ] = part

    weight_copy(0).wait()
    weight_copy(1).wait()
    weight_copy(2).wait()
    weight_copy(3).wait()
    weight_copy(4).wait()
    wait_units(0, BLOCK, 0)
    compute(0)

    pl.semaphore_wait(barrier, RANKS - 1 + X_DEV - 1 + Y_DEV - 1)

    def rows_of(c):
        return pl.ds(c * CHUNK, CHUNK)

    def y_copy(step, c):
        return pltpu.make_async_remote_copy(
            src_ref=docs.at[:, :, rows_of(c)],
            dst_ref=recv1[c].at[pl.ds(me_y * GROUP_DEV, GROUP_DEV)],
            send_sem=y_send.at[c, step - 1],
            recv_sem=y_recv.at[c, step - 1],
            device_id={"dp": y_peer(step), "tensor": me_t},
            device_id_type=MESH,
        )

    for c in range(CHUNKS):
        for step in (2, 1, 3):
            y_copy(step, c).start()

    def own_copy(c):
        return pltpu.make_async_copy(
            docs.at[:, :, rows_of(c)],
            recv1[c].at[pl.ds(me_y * GROUP_DEV, GROUP_DEV)],
            own_sem.at[c],
        )

    for c in range(CHUNKS):
        own_copy(c).start()

    wait_units(BLOCK, UNITS - BLOCK, 1)
    for block in range(1, UNITS // BLOCK):
        compute(block)

    mine = pl.ds(me_t * 2, 2)

    def to_rank(rank, source, target, send, recv):
        return pltpu.make_async_remote_copy(
            src_ref=source,
            dst_ref=target,
            send_sem=send.at[rank],
            recv_sem=recv.at[me_t],
            device_id={"dp": me_dp, "tensor": rank},
            device_id_type=MESH,
        )

    def whole(rank, source):
        return to_rank(rank, source, out_ref.at[mine], t_send, t_recv)

    def head_part(rank, source):
        return to_rank(rank, source, out_ref.at[mine, pl.ds(0, HALF)], h_send, h_recv)

    def tail_part(rank, source):
        return to_rank(
            rank, source, out_ref.at[mine, pl.ds(HALF, OWN_ROWS - HALF)], t_send, t_recv
        )

    def front_rows(rank):
        return front.at[rank // SHARE, :, pl.ds(lax.rem(rank, SHARE) * OWN_ROWS, OWN_ROWS)]

    def front_end(rank):
        return front.at[rank // SHARE, :, pl.ds(TAIL, HALF)]

    def final_rows(rank):
        start = (lax.rem(rank, SHARE) - CUT) * OWN_ROWS - HALF
        return final.at[rank // SHARE, :, pl.ds(start, OWN_ROWS)]

    def final_start(rank):
        return final.at[rank // SHARE, :, pl.ds(0, OWN_ROWS - HALF)]

    def send_front(step, carry):
        rank = lax.rem(me_t + step, RANKS)
        place = lax.rem(rank, SHARE)

        @pl.when(place < CUT)
        def _():
            whole(rank, front_rows(rank)).start()

        @pl.when(place == CUT)
        def _():
            head_part(rank, front_end(rank)).start()

        return carry

    lax.fori_loop(1, RANKS, send_front, 0)
    my_place = lax.rem(me_t, SHARE)

    @pl.when(my_place < CUT)
    def _():
        pltpu.make_async_copy(front_rows(me_t), out_ref.at[mine], local_sem.at[1]).start()

    @pl.when(my_place == CUT)
    def _():
        pltpu.make_async_copy(
            front_end(me_t), out_ref.at[mine, pl.ds(0, HALF)], local_sem.at[2]
        ).start()

    even = lax.broadcasted_iota(jnp.int32, (CHUNK, V_HEAD), 0) % MB == 0

    def build(c):
        at = slice(c * CHUNK, (c + 1) * CHUNK)
        for step in range(X_DEV):
            x_at = lax.rem(me_x + step, X_DEV)
            for j in range(GROUP_DEV):
                group = (me_y * X_DEV + x_at) * GROUP_DEV + j
                index = []
                for m in range(MB):
                    mate = partner_ref[m, group]
                    index.append(mate // (X_DEV * GROUP_DEV) * GROUP_DEV + mate % GROUP_DEV)
                for h in range(2):
                    picked = jnp.where(
                        even, recv1[c][index[0], h], recv1[c][index[1], h]
                    )
                    if step == 0:
                        recv2[c][me_x, j, h] = picked
                    else:
                        snd2[step - 1, j, h, at, :] = picked

    def x_copy(step, c):
        return pltpu.make_async_remote_copy(
            src_ref=snd2.at[step - 1, :, :, rows_of(c)],
            dst_ref=recv2[c].at[me_x],
            send_sem=x_send.at[c, step - 1],
            recv_sem=x_recv.at[c, step - 1],
            device_id={"dp": x_peer(step), "tensor": me_t},
            device_id_type=MESH,
        )

    def first_half(c):
        own_copy(c).wait()
        for step in range(1, Y_DEV):
            y_copy(step, c).wait_recv()
        build(c)
        for step in (2, 1, 3):
            x_copy(step, c).start()

    def second_half(c):
        for step in range(1, X_DEV):
            x_copy(step, c).wait_recv()
        at = slice(c * CHUNK // MB, (c + 1) * CHUNK // MB)
        for j in range(GROUP_DEV):
            group = me_dp * GROUP_DEV + j
            source = []
            light = []
            for m in range(MB):
                source.append((partner_ref[m, group] // GROUP_DEV) % X_DEV)
                live = jnp.int32(0)
                for s in range(SLOTS):
                    live += (len_ref[m, group * SLOTS + s] > 0).astype(jnp.int32)
                light.append(live < SLOTS)
            for h in range(2):
                picks = [
                    jnp.where(light[m], recv2[c][source[m], j, h], jnp.zeros((), BF16))
                    for m in range(MB)
                ]
                value = jnp.where(even, picks[0], picks[1])
                final[j, h, at] = value.reshape(CHUNK // MB, MB, V_HEAD)
        low = CUT + 2 * c
        for place in (low, low + 1):

            def send_final(step, carry, place=place):
                rank = lax.rem(me_t // SHARE + step, GROUP_DEV) * SHARE + place

                @pl.when(rank != me_t)
                def _():
                    if place == CUT:
                        tail_part(rank, final_start(rank)).start()
                    else:
                        whole(rank, final_rows(rank)).start()

                return carry

            lax.fori_loop(0, GROUP_DEV, send_final, 0)

    first_half(0)
    first_half(1)
    second_half(0)
    first_half(2)
    second_half(1)
    second_half(2)

    @pl.when(my_place == CUT)
    def _():
        pltpu.make_async_copy(
            final_start(me_t), out_ref.at[mine, pl.ds(HALF, OWN_ROWS - HALF)], local_sem.at[1]
        ).start()

    @pl.when(my_place > CUT)
    def _():
        pltpu.make_async_copy(final_rows(me_t), out_ref.at[mine], local_sem.at[1]).start()

    def await_recv(step, carry):
        source = lax.rem(me_t + step, RANKS)
        theirs = pl.ds(source * 2, 2)

        def arrived(rows, recv):
            part = out_ref.at[theirs, rows]
            pltpu.make_async_copy(part, part, recv.at[source]).wait()

        @pl.when(my_place == CUT)
        def _():
            arrived(pl.ds(0, HALF), h_recv)
            arrived(pl.ds(HALF, OWN_ROWS - HALF), t_recv)

        @pl.when(my_place != CUT)
        def _():
            arrived(pl.ds(0, OWN_ROWS), t_recv)

        return carry

    def await_send(step, carry):
        rank = lax.rem(me_t + step, RANKS)
        place = lax.rem(rank, SHARE)

        @pl.when(place == CUT)
        def _():
            head_part(rank, front_end(rank)).wait_send()
            tail_part(rank, final_start(rank)).wait_send()

        @pl.when(place != CUT)
        def _():
            whole(rank, front.at[0, :, pl.ds(0, OWN_ROWS)]).wait_send()

        return carry

    lax.fori_loop(1, RANKS, await_send, 0)
    for c in range(CHUNKS):
        for step in range(1, Y_DEV):
            y_copy(step, c).wait_send()
        for step in range(1, X_DEV):
            x_copy(step, c).wait_send()

    @pl.when(my_place == CUT)
    def _():
        pltpu.make_async_copy(
            front_end(me_t), out_ref.at[mine, pl.ds(0, HALF)], local_sem.at[2]
        ).wait()
        pltpu.make_async_copy(
            final_start(me_t), out_ref.at[mine, pl.ds(HALF, OWN_ROWS - HALF)], local_sem.at[1]
        ).wait()

    @pl.when(my_place != CUT)
    def _():
        pltpu.make_async_copy(
            front.at[0, :, pl.ds(0, OWN_ROWS)], out_ref.at[mine], local_sem.at[1]
        ).wait()

    lax.fori_loop(1, RANKS, await_recv, 0)


def attend(
    partner, doc_length, query, key, up_query, up_rope, key_absorb, value_expand
):
    smem = pl.BlockSpec(memory_space=pltpu.SMEM)
    anyw = pl.BlockSpec(memory_space=pl.ANY)
    part = (GROUP_DEV, 2, PAIR, V_HEAD)
    return pl.pallas_call(
        kernel,
        out_shape=jax.ShapeDtypeStruct((RANKS * 2, OWN_ROWS, MB, V_HEAD), BF16),
        in_specs=[smem, smem] + [anyw] * 7,
        out_specs=anyw,
        scratch_shapes=[
            pltpu.VMEM((UNITS * PAIR, Q_RANK), BF16),
            pltpu.VMEM((UNITS * PAIR, KV_RANK + ROPE), BF16),
            pltpu.VMEM((Q_RANK, 2 * NOPE), BF16),
            pltpu.VMEM((Q_RANK, 2 * ROPE), BF16),
            pltpu.VMEM((2 * NOPE, KV_RANK), BF16),
            pltpu.VMEM((KV_RANK, 2 * V_HEAD), BF16),
            pltpu.VMEM((2, PAIR, 128), jnp.float32),
            pltpu.VMEM((GROUP_DEV, 2, (SLOTS - 1) * DOC, MB, V_HEAD), BF16),
            pltpu.VMEM(part, BF16),
            *[pltpu.VMEM((Y_DEV * GROUP_DEV, 2, CHUNK, V_HEAD), BF16)] * CHUNKS,
            pltpu.VMEM((X_DEV - 1,) + part, BF16),
            *[pltpu.VMEM((X_DEV, GROUP_DEV, 2, CHUNK, V_HEAD), BF16)] * CHUNKS,
            pltpu.VMEM((GROUP_DEV, 2, DOC, MB, V_HEAD), BF16),
            pltpu.SemaphoreType.DMA((9,)),
            pltpu.SemaphoreType.DMA((3,)),
            pltpu.SemaphoreType.DMA((CHUNKS,)),
            pltpu.SemaphoreType.DMA((CHUNKS, Y_DEV - 1)),
            pltpu.SemaphoreType.DMA((CHUNKS, Y_DEV - 1)),
            pltpu.SemaphoreType.DMA((CHUNKS, X_DEV - 1)),
            pltpu.SemaphoreType.DMA((CHUNKS, X_DEV - 1)),
            pltpu.SemaphoreType.DMA((RANKS,)),
            pltpu.SemaphoreType.DMA((RANKS,)),
            pltpu.SemaphoreType.DMA((RANKS,)),
            pltpu.SemaphoreType.DMA((RANKS,)),
        ],
        compiler_params=pltpu.CompilerParams(collective_id=0, has_side_effects=True),
        name="attend",
    )(
        partner,
        doc_length,
        query,
        key,
        up_query,
        up_rope,
        key_absorb,
        value_expand,
        jnp.asarray(rope_tables()),
    )


def body(
    query_latent, key_latent, partner, doc_length, up_query, up_rope, key_absorb, value_expand
):
    result = attend(
        partner,
        doc_length,
        query_latent,
        key_latent,
        up_query,
        up_rope,
        key_absorb,
        value_expand,
    )
    return result.transpose(2, 1, 0, 3).reshape(MB, OWN_ROWS, RANKS * 2 * V_HEAD)


def solution(mesh):
    in_specs = (
        P(None, "dp", None),
        P(None, "dp", None),
        P(),
        P(),
        P(None, "tensor"),
        P(None, "tensor"),
        P("tensor", None),
        P(None, "tensor"),
    )
    out_specs = P(None, ("dp", "tensor"), None)
    return jax.shard_map(body, mesh=mesh, in_specs=in_specs, out_specs=out_specs, check_vma=False)
```

```python
import jax
import jax.numpy as jnp
import numpy as np
from jax import lax
from jax.experimental import pallas as pl
from jax.experimental.pallas import tpu as pltpu
from jax.sharding import PartitionSpec as P

Q_RANK = 1536
KV_RANK = 512
ROPE = 64
NOPE = 128
V_HEAD = 128
DOC = 48
SLOTS = 3
GROUP_DEV = 3
ROWS = SLOTS * DOC
MB = 2
PAIR = MB * DOC
UNITS = GROUP_DEV * SLOTS
BLOCK = 3
MESH = pl.DeviceIdType.MESH
X_DEV = 4
Y_DEV = 4
RANKS = 48
OWN_ROWS = 9
SHARE = ROWS // OWN_ROWS
CUT = 10
TAIL = CUT * OWN_ROWS
HALF = (SLOTS - 1) * DOC - TAIL
CHUNKS = 4
PLACES = ((CUT, CUT + 1), (CUT + 2,), (CUT + 3,), (CUT + 4, CUT + 5))
CHUNK = PAIR // CHUNKS
BF16 = jnp.bfloat16


def rope_tables():
    freq = 10000.0 ** (-np.arange(32, dtype=np.float32) / np.float32(32))
    angles = np.arange(DOC, dtype=np.float32)[:, None] * freq.astype(np.float32)[None, :]
    cosine = np.cos(angles.astype(np.float64)).astype(np.float32)
    sine = np.sin(angles.astype(np.float64)).astype(np.float32)
    cos_row = np.concatenate([cosine] * 4, 1)
    sin_row = np.concatenate([-sine, sine, -sine, sine], 1)
    return np.stack([np.concatenate([t] * MB, 0) for t in (cos_row, sin_row)])


def dot(a, b, dims=((1,), (0,))):
    return lax.dot_general(a, b, (dims, ((), ())), preferred_element_type=jnp.float32)


def rotate_pairs(values, cosine, sine):
    lane = lax.broadcasted_iota(jnp.int32, values.shape, 1)
    swapped = jnp.where(
        lane % 64 < 32, pltpu.roll(values, 96, 1), pltpu.roll(values, 32, 1)
    )
    return values * cosine + swapped * sine


def unit_place(unit):
    if unit < GROUP_DEV:
        return unit, SLOTS - 1
    return (unit - GROUP_DEV) // (SLOTS - 1), (unit - GROUP_DEV) % (SLOTS - 1)


def kernel(
    partner_ref,
    len_ref,
    q_ref,
    k_ref,
    uq_ref,
    ur_ref,
    ab_ref,
    ve_ref,
    tab_ref,
    out_ref,
    xbuf,
    kbuf,
    uq,
    ur,
    ab,
    ve,
    tab,
    front,
    docs,
    recv1_a,
    recv1_b,
    recv1_c,
    recv1_d,
    snd2,
    recv2_a,
    recv2_b,
    recv2_c,
    recv2_d,
    final,
    load_sem,
    local_sem,
    own_sem,
    y_send,
    y_recv,
    x_send,
    x_recv,
    t_send,
    t_recv,
    h_send,
    h_recv,
):
    recv1 = (recv1_a, recv1_b, recv1_c, recv1_d)
    recv2 = (recv2_a, recv2_b, recv2_c, recv2_d)
    me_dp = lax.axis_index("dp")
    me_t = lax.axis_index("tensor")
    me_x = me_dp % X_DEV
    me_y = me_dp // X_DEV

    def y_peer(step):
        return lax.rem(me_y + step, Y_DEV) * X_DEV + me_x

    def x_peer(step):
        return me_y * X_DEV + lax.rem(me_x + step, X_DEV)

    def load_units(units, half):
        for unit in units:
            j, s = unit_place(unit)
            rows = pl.ds(j * ROWS + s * DOC, DOC)
            for m in range(MB):
                at = pl.ds(unit * PAIR + m * DOC, DOC)
                pltpu.make_async_copy(q_ref.at[m, rows], xbuf.at[at], load_sem.at[half]).start()
                pltpu.make_async_copy(k_ref.at[m, rows], kbuf.at[at], load_sem.at[2 + half]).start()

    def wait_units(first, count, half):
        at = pl.ds(first * PAIR, count * PAIR)
        pltpu.make_async_copy(xbuf.at[at], xbuf.at[at], load_sem.at[half]).wait()
        pltpu.make_async_copy(kbuf.at[at], kbuf.at[at], load_sem.at[2 + half]).wait()

    weights = ((uq_ref, uq), (ur_ref, ur), (tab_ref, tab), (ab_ref, ab), (ve_ref, ve))

    def weight_copy(n):
        return pltpu.make_async_copy(weights[n][0], weights[n][1], load_sem.at[4 + n])

    weight_copy(0).start()
    load_units(range(BLOCK), 0)
    for n in range(1, 5):
        weight_copy(n).start()
    load_units(range(BLOCK, UNITS), 1)

    barrier = pltpu.get_barrier_semaphore()

    def greet(step, carry):
        pl.semaphore_signal(
            barrier,
            inc=1,
            device_id={"dp": me_dp, "tensor": lax.rem(me_t + step, RANKS)},
            device_id_type=MESH,
        )
        return carry

    lax.fori_loop(1, RANKS, greet, 0)
    for step in range(1, Y_DEV):
        pl.semaphore_signal(
            barrier, inc=1, device_id={"dp": y_peer(step), "tensor": me_t}, device_id_type=MESH
        )
    for step in range(1, X_DEV):
        pl.semaphore_signal(
            barrier, inc=1, device_id={"dp": x_peer(step), "tensor": me_t}, device_id_type=MESH
        )

    scale = (NOPE + ROPE) ** -0.5
    perm_row = lax.broadcasted_iota(jnp.int32, (PAIR, PAIR), 0)
    perm_col = lax.broadcasted_iota(jnp.int32, (PAIR, PAIR), 1)
    perm = (perm_col == (perm_row % MB) * DOC + perm_row // MB).astype(jnp.float32).astype(BF16)
    row_at = lax.broadcasted_iota(jnp.int32, (2 * PAIR, PAIR), 0) % PAIR
    row_micro = row_at % MB
    row_pos = row_at // MB
    key_at = lax.broadcasted_iota(jnp.int32, (2 * PAIR, PAIR), 1)
    key_pos = key_at % DOC
    causal = (key_at // DOC == row_micro) & (key_pos <= row_pos)
    diagonal = key_pos == row_pos
    out_at = lax.broadcasted_iota(jnp.int32, (PAIR, V_HEAD), 0)
    lane = lax.broadcasted_iota(jnp.int32, (PAIR, 128), 1)
    head_lane = [(lane // ROPE == h).astype(jnp.float32).astype(BF16) for h in range(2)]

    def compute(block):
        rows = slice(block * BLOCK * PAIR, (block + 1) * BLOCK * PAIR)
        x = xbuf[rows, :]
        nope = dot(x, uq[...]).astype(BF16)
        rope = dot(x, ur[...])
        mixed_all = [[], []]
        ordered = []
        for i in range(BLOCK):
            at = slice(i * PAIR, (i + 1) * PAIR)
            turned = rotate_pairs(rope[at], tab[0], tab[1]).astype(BF16)
            both = jnp.concatenate([nope[at], turned], 1)
            ordered.append(dot(perm, both).astype(BF16))
        ordered = jnp.concatenate(ordered, 0)
        absorbed = [
            dot(ordered[:, h * NOPE : (h + 1) * NOPE], ab[h * NOPE : (h + 1) * NOPE, :]).astype(BF16)
            for h in range(2)
        ]
        lengths = []
        for i in range(BLOCK):
            unit = block * BLOCK + i
            j, s = unit_place(unit)
            at = slice(i * PAIR, (i + 1) * PAIR)
            here = slice(unit * PAIR, (unit + 1) * PAIR)
            latent = kbuf[here, 0:KV_RANK]
            kr = kbuf[here, KV_RANK : KV_RANK + ROPE].astype(jnp.float32)
            kr = rotate_pairs(jnp.concatenate([kr, kr], 1), tab[0], tab[1]).astype(BF16)
            keys = jnp.concatenate([latent, kr], 1)
            qr = ordered[at, 2 * NOPE :]
            queries = jnp.concatenate(
                [
                    jnp.concatenate([absorbed[h][at], qr * head_lane[h]], 1)
                    for h in range(2)
                ],
                0,
            )
            scores = dot(queries, keys, ((1,), (1,)))
            slot = (me_dp * GROUP_DEV + j) * SLOTS + s
            pair_len = [len_ref[m, slot] for m in range(MB)]
            lengths.append(pair_len)
            live = jnp.where(row_micro == 0, pair_len[0], pair_len[1])
            allowed = causal & ((key_pos < live) | diagonal)
            scores = jnp.where(allowed, scores * scale, -jnp.inf)
            weight = jnp.exp(scores - jnp.max(scores, 1, keepdims=True))
            prob = (weight / jnp.sum(weight, 1, keepdims=True)).astype(BF16)
            mixed = dot(prob, latent).astype(BF16)
            for h in range(2):
                mixed_all[h].append(mixed[h * PAIR : (h + 1) * PAIR])
        for h in range(2):
            res = dot(jnp.concatenate(mixed_all[h], 0), ve[:, h * V_HEAD : (h + 1) * V_HEAD])
            for i in range(BLOCK):
                j, s = unit_place(block * BLOCK + i)
                live = jnp.where(out_at % MB == 0, lengths[i][0], lengths[i][1])
                part = jnp.where(out_at // MB < live, res[i * PAIR : (i + 1) * PAIR], 0.0)
                part = part.astype(BF16)
                if block == 0:
                    docs[j, h] = part
                else:
                    front.at[j, h].reshape((SLOTS - 1) * PAIR, V_HEAD)[
                        s * PAIR : (s + 1) * PAIR, :
                    ] = part

    weight_copy(0).wait()
    weight_copy(1).wait()
    weight_copy(2).wait()
    weight_copy(3).wait()
    weight_copy(4).wait()
    wait_units(0, BLOCK, 0)
    compute(0)

    pl.semaphore_wait(barrier, RANKS - 1 + X_DEV - 1 + Y_DEV - 1)

    def rows_of(c):
        return pl.ds(c * CHUNK, CHUNK)

    def y_copy(step, c):
        return pltpu.make_async_remote_copy(
            src_ref=docs.at[:, :, rows_of(c)],
            dst_ref=recv1[c].at[pl.ds(me_y * GROUP_DEV, GROUP_DEV)],
            send_sem=y_send.at[c, step - 1],
            recv_sem=y_recv.at[c, step - 1],
            device_id={"dp": y_peer(step), "tensor": me_t},
            device_id_type=MESH,
        )

    def relay(c):
        step, back = (1, 3) if c % 2 == 0 else (3, 1)
        slots = pl.ds(lax.rem(me_y + back, Y_DEV) * GROUP_DEV, GROUP_DEV)
        return pltpu.make_async_remote_copy(
            src_ref=recv1[c].at[slots],
            dst_ref=recv1[c].at[slots],
            send_sem=y_send.at[c, 1],
            recv_sem=y_recv.at[c, 1],
            device_id={"dp": y_peer(step), "tensor": me_t},
            device_id_type=MESH,
        )

    def pass_on(c):
        y_copy(1 if c % 2 == 0 else 3, c).wait_recv()
        relay(c).start()

    for step, c in ((1, 0), (3, 1), (1, 2), (3, 3), (1, 1), (3, 0), (1, 3), (3, 2)):
        y_copy(step, c).start()

    def own_copy(c):
        return pltpu.make_async_copy(
            docs.at[:, :, rows_of(c)],
            recv1[c].at[pl.ds(me_y * GROUP_DEV, GROUP_DEV)],
            own_sem.at[c],
        )

    for c in range(CHUNKS):
        own_copy(c).start()

    wait_units(BLOCK, UNITS - BLOCK, 1)
    compute(1)
    pass_on(0)
    pass_on(1)
    compute(2)
    pass_on(2)
    pass_on(3)

    mine = pl.ds(me_t * 2, 2)

    def to_rank(rank, source, target, send, recv):
        return pltpu.make_async_remote_copy(
            src_ref=source,
            dst_ref=target,
            send_sem=send.at[rank],
            recv_sem=recv.at[me_t],
            device_id={"dp": me_dp, "tensor": rank},
            device_id_type=MESH,
        )

    def whole(rank, source):
        return to_rank(rank, source, out_ref.at[mine], t_send, t_recv)

    def head_part(rank, source):
        return to_rank(rank, source, out_ref.at[mine, pl.ds(0, HALF)], h_send, h_recv)

    def tail_part(rank, source):
        return to_rank(
            rank, source, out_ref.at[mine, pl.ds(HALF, OWN_ROWS - HALF)], t_send, t_recv
        )

    def front_rows(rank):
        return front.at[rank // SHARE, :, pl.ds(lax.rem(rank, SHARE) * OWN_ROWS, OWN_ROWS)]

    def front_end(rank):
        return front.at[rank // SHARE, :, pl.ds(TAIL, HALF)]

    def final_rows(rank):
        start = (lax.rem(rank, SHARE) - CUT) * OWN_ROWS - HALF
        return final.at[rank // SHARE, :, pl.ds(start, OWN_ROWS)]

    def final_start(rank):
        return final.at[rank // SHARE, :, pl.ds(0, OWN_ROWS - HALF)]

    def send_front(step, carry):
        offset = RANKS // 2 + (1 - 2 * (step % 2)) * (step // 2)
        rank = lax.rem(me_t + offset, RANKS)
        place = lax.rem(rank, SHARE)

        @pl.when(place < CUT)
        def _():
            whole(rank, front_rows(rank)).start()

        @pl.when(place == CUT)
        def _():
            head_part(rank, front_end(rank)).start()

        return carry

    lax.fori_loop(1, RANKS, send_front, 0)
    my_place = lax.rem(me_t, SHARE)

    @pl.when(my_place < CUT)
    def _():
        pltpu.make_async_copy(front_rows(me_t), out_ref.at[mine], local_sem.at[1]).start()

    @pl.when(my_place == CUT)
    def _():
        pltpu.make_async_copy(
            front_end(me_t), out_ref.at[mine, pl.ds(0, HALF)], local_sem.at[2]
        ).start()

    even = lax.broadcasted_iota(jnp.int32, (CHUNK, V_HEAD), 0) % MB == 0

    def build(c):
        at = slice(c * CHUNK, (c + 1) * CHUNK)
        for step in range(X_DEV):
            x_at = lax.rem(me_x + step, X_DEV)
            for j in range(GROUP_DEV):
                group = (me_y * X_DEV + x_at) * GROUP_DEV + j
                index = []
                for m in range(MB):
                    mate = partner_ref[m, group]
                    index.append(mate // (X_DEV * GROUP_DEV) * GROUP_DEV + mate % GROUP_DEV)
                for h in range(2):
                    picked = jnp.where(
                        even, recv1[c][index[0], h], recv1[c][index[1], h]
                    )
                    if step == 0:
                        recv2[c][me_x, j, h] = picked
                    else:
                        snd2[step - 1, j, h, at, :] = picked

    def x_copy(step, c):
        return pltpu.make_async_remote_copy(
            src_ref=snd2.at[step - 1, :, :, rows_of(c)],
            dst_ref=recv2[c].at[me_x],
            send_sem=x_send.at[c, step - 1],
            recv_sem=x_recv.at[c, step - 1],
            device_id={"dp": x_peer(step), "tensor": me_t},
            device_id_type=MESH,
        )

    def first_half(c):
        own_copy(c).wait()
        y_copy(3 if c % 2 == 0 else 1, c).wait_recv()
        relay(c).wait_recv()
        build(c)
        for step in (2, 1, 3):
            x_copy(step, c).start()

    def second_half(c):
        for step in range(1, X_DEV):
            x_copy(step, c).wait_recv()
        at = slice(c * CHUNK // MB, (c + 1) * CHUNK // MB)
        for j in range(GROUP_DEV):
            group = me_dp * GROUP_DEV + j
            source = []
            light = []
            for m in range(MB):
                source.append((partner_ref[m, group] // GROUP_DEV) % X_DEV)
                live = jnp.int32(0)
                for s in range(SLOTS):
                    live += (len_ref[m, group * SLOTS + s] > 0).astype(jnp.int32)
                light.append(live < SLOTS)
            for h in range(2):
                picks = [
                    jnp.where(light[m], recv2[c][source[m], j, h], jnp.zeros((), BF16))
                    for m in range(MB)
                ]
                value = jnp.where(even, picks[0], picks[1])
                final[j, h, at] = value.reshape(CHUNK // MB, MB, V_HEAD)
        for place in PLACES[c]:

            def send_final(step, carry, place=place):
                rank = lax.rem(me_t // SHARE + step, GROUP_DEV) * SHARE + place

                @pl.when(rank != me_t)
                def _():
                    if place == CUT:
                        tail_part(rank, final_start(rank)).start()
                    else:
                        whole(rank, final_rows(rank)).start()

                return carry

            lax.fori_loop(0, GROUP_DEV, send_final, 0)

    first_half(0)
    first_half(1)
    second_half(0)
    first_half(2)
    second_half(1)
    first_half(3)
    second_half(2)
    second_half(3)

    @pl.when(my_place == CUT)
    def _():
        pltpu.make_async_copy(
            final_start(me_t), out_ref.at[mine, pl.ds(HALF, OWN_ROWS - HALF)], local_sem.at[1]
        ).start()

    @pl.when(my_place > CUT)
    def _():
        pltpu.make_async_copy(final_rows(me_t), out_ref.at[mine], local_sem.at[1]).start()

    def await_recv(step, carry):
        source = lax.rem(me_t + step, RANKS)
        theirs = pl.ds(source * 2, 2)

        def arrived(rows, recv):
            part = out_ref.at[theirs, rows]
            pltpu.make_async_copy(part, part, recv.at[source]).wait()

        @pl.when(my_place == CUT)
        def _():
            arrived(pl.ds(0, HALF), h_recv)
            arrived(pl.ds(HALF, OWN_ROWS - HALF), t_recv)

        @pl.when(my_place != CUT)
        def _():
            arrived(pl.ds(0, OWN_ROWS), t_recv)

        return carry

    def await_send(step, carry):
        rank = lax.rem(me_t + step, RANKS)
        place = lax.rem(rank, SHARE)

        @pl.when(place == CUT)
        def _():
            head_part(rank, front_end(rank)).wait_send()
            tail_part(rank, final_start(rank)).wait_send()

        @pl.when(place != CUT)
        def _():
            whole(rank, front.at[0, :, pl.ds(0, OWN_ROWS)]).wait_send()

        return carry

    lax.fori_loop(1, RANKS, await_send, 0)
    for c in range(CHUNKS):
        for step in (1, 3):
            y_copy(step, c).wait_send()
        relay(c).wait_send()
        for step in range(1, X_DEV):
            x_copy(step, c).wait_send()

    @pl.when(my_place == CUT)
    def _():
        pltpu.make_async_copy(
            front_end(me_t), out_ref.at[mine, pl.ds(0, HALF)], local_sem.at[2]
        ).wait()
        pltpu.make_async_copy(
            final_start(me_t), out_ref.at[mine, pl.ds(HALF, OWN_ROWS - HALF)], local_sem.at[1]
        ).wait()

    @pl.when(my_place != CUT)
    def _():
        pltpu.make_async_copy(
            front.at[0, :, pl.ds(0, OWN_ROWS)], out_ref.at[mine], local_sem.at[1]
        ).wait()

    lax.fori_loop(1, RANKS, await_recv, 0)


def attend(
    partner, doc_length, query, key, up_query, up_rope, key_absorb, value_expand
):
    smem = pl.BlockSpec(memory_space=pltpu.SMEM)
    anyw = pl.BlockSpec(memory_space=pl.ANY)
    part = (GROUP_DEV, 2, PAIR, V_HEAD)
    return pl.pallas_call(
        kernel,
        out_shape=jax.ShapeDtypeStruct((RANKS * 2, OWN_ROWS, MB, V_HEAD), BF16),
        in_specs=[smem, smem] + [anyw] * 7,
        out_specs=anyw,
        scratch_shapes=[
            pltpu.VMEM((UNITS * PAIR, Q_RANK), BF16),
            pltpu.VMEM((UNITS * PAIR, KV_RANK + ROPE), BF16),
            pltpu.VMEM((Q_RANK, 2 * NOPE), BF16),
            pltpu.VMEM((Q_RANK, 2 * ROPE), BF16),
            pltpu.VMEM((2 * NOPE, KV_RANK), BF16),
            pltpu.VMEM((KV_RANK, 2 * V_HEAD), BF16),
            pltpu.VMEM((2, PAIR, 128), jnp.float32),
            pltpu.VMEM((GROUP_DEV, 2, (SLOTS - 1) * DOC, MB, V_HEAD), BF16),
            pltpu.VMEM(part, BF16),
            *[pltpu.VMEM((Y_DEV * GROUP_DEV, 2, CHUNK, V_HEAD), BF16)] * CHUNKS,
            pltpu.VMEM((X_DEV - 1,) + part, BF16),
            *[pltpu.VMEM((X_DEV, GROUP_DEV, 2, CHUNK, V_HEAD), BF16)] * CHUNKS,
            pltpu.VMEM((GROUP_DEV, 2, DOC, MB, V_HEAD), BF16),
            pltpu.SemaphoreType.DMA((9,)),
            pltpu.SemaphoreType.DMA((3,)),
            pltpu.SemaphoreType.DMA((CHUNKS,)),
            pltpu.SemaphoreType.DMA((CHUNKS, Y_DEV - 1)),
            pltpu.SemaphoreType.DMA((CHUNKS, Y_DEV - 1)),
            pltpu.SemaphoreType.DMA((CHUNKS, X_DEV - 1)),
            pltpu.SemaphoreType.DMA((CHUNKS, X_DEV - 1)),
            pltpu.SemaphoreType.DMA((RANKS,)),
            pltpu.SemaphoreType.DMA((RANKS,)),
            pltpu.SemaphoreType.DMA((RANKS,)),
            pltpu.SemaphoreType.DMA((RANKS,)),
        ],
        compiler_params=pltpu.CompilerParams(collective_id=0, has_side_effects=True),
        name="attend",
    )(
        partner,
        doc_length,
        query,
        key,
        up_query,
        up_rope,
        key_absorb,
        value_expand,
        jnp.asarray(rope_tables()),
    )


def body(
    query_latent, key_latent, partner, doc_length, up_query, up_rope, key_absorb, value_expand
):
    result = attend(
        partner,
        doc_length,
        query_latent,
        key_latent,
        up_query,
        up_rope,
        key_absorb,
        value_expand,
    )
    return result.transpose(2, 1, 0, 3).reshape(MB, OWN_ROWS, RANKS * 2 * V_HEAD)


def solution(mesh):
    in_specs = (
        P(None, "dp", None),
        P(None, "dp", None),
        P(),
        P(),
        P(None, "tensor"),
        P(None, "tensor"),
        P("tensor", None),
        P(None, "tensor"),
    )
    out_specs = P(None, ("dp", "tensor"), None)
    return jax.shard_map(body, mesh=mesh, in_specs=in_specs, out_specs=out_specs, check_vma=False)
```

```python
import jax
import jax.numpy as jnp
import numpy as np
from jax import lax
from jax.experimental import pallas as pl
from jax.experimental.pallas import tpu as pltpu
from jax.sharding import PartitionSpec as P

Q_RANK = 1536
KV_RANK = 512
ROPE = 64
NOPE = 128
V_HEAD = 128
DOC = 48
SLOTS = 3
GROUP_DEV = 3
ROWS = SLOTS * DOC
MB = 2
PAIR = MB * DOC
UNITS = GROUP_DEV * SLOTS
BLOCK = 3
MESH = pl.DeviceIdType.MESH
X_DEV = 4
Y_DEV = 4
RANKS = 48
OWN_ROWS = 9
SHARE = ROWS // OWN_ROWS
CUT = 10
TAIL = CUT * OWN_ROWS
HALF = (SLOTS - 1) * DOC - TAIL
CHUNKS = 4
PLACES = ((CUT, CUT + 1), (CUT + 2,), (CUT + 3,), (CUT + 4, CUT + 5))
CHUNK = PAIR // CHUNKS
BF16 = jnp.bfloat16


def rope_tables():
    freq = 10000.0 ** (-np.arange(32, dtype=np.float32) / np.float32(32))
    angles = np.arange(DOC, dtype=np.float32)[:, None] * freq.astype(np.float32)[None, :]
    cosine = np.cos(angles.astype(np.float64)).astype(np.float32)
    sine = np.sin(angles.astype(np.float64)).astype(np.float32)
    cos_row = np.concatenate([cosine] * 4, 1)
    sin_row = np.concatenate([-sine, sine, -sine, sine], 1)
    return np.stack([np.concatenate([t] * MB, 0) for t in (cos_row, sin_row)])


def dot(a, b, dims=((1,), (0,))):
    return lax.dot_general(a, b, (dims, ((), ())), preferred_element_type=jnp.float32)


def rotate_pairs(values, cosine, sine):
    lane = lax.broadcasted_iota(jnp.int32, values.shape, 1)
    swapped = jnp.where(
        lane % 64 < 32, pltpu.roll(values, 96, 1), pltpu.roll(values, 32, 1)
    )
    return values * cosine + swapped * sine


def unit_place(unit):
    if unit < GROUP_DEV:
        return unit, SLOTS - 1
    return (unit - GROUP_DEV) // (SLOTS - 1), (unit - GROUP_DEV) % (SLOTS - 1)


def kernel(
    partner_ref,
    len_ref,
    q_ref,
    k_ref,
    uq_ref,
    ur_ref,
    ab_ref,
    ve_ref,
    tab_ref,
    out_ref,
    xbuf,
    kbuf,
    uq,
    ur,
    ab,
    ve,
    tab,
    front,
    docs,
    recv1_a,
    recv1_b,
    recv1_c,
    recv1_d,
    snd2,
    recv2_a,
    recv2_b,
    recv2_c,
    recv2_d,
    final,
    load_sem,
    local_sem,
    own_sem,
    y_send,
    y_recv,
    x_send,
    x_recv,
    t_send,
    t_recv,
    h_send,
    h_recv,
):
    recv1 = (recv1_a, recv1_b, recv1_c, recv1_d)
    recv2 = (recv2_a, recv2_b, recv2_c, recv2_d)
    me_dp = lax.axis_index("dp")
    me_t = lax.axis_index("tensor")
    me_x = me_dp % X_DEV
    me_y = me_dp // X_DEV

    def y_peer(step):
        return lax.rem(me_y + step, Y_DEV) * X_DEV + me_x

    def x_peer(step):
        return me_y * X_DEV + lax.rem(me_x + step, X_DEV)

    def load_units(units, half):
        for unit in units:
            j, s = unit_place(unit)
            rows = pl.ds(j * ROWS + s * DOC, DOC)
            for m in range(MB):
                at = pl.ds(unit * PAIR + m * DOC, DOC)
                pltpu.make_async_copy(q_ref.at[m, rows], xbuf.at[at], load_sem.at[half]).start()
                pltpu.make_async_copy(k_ref.at[m, rows], kbuf.at[at], load_sem.at[2 + half]).start()

    def wait_units(first, count, half):
        at = pl.ds(first * PAIR, count * PAIR)
        pltpu.make_async_copy(xbuf.at[at], xbuf.at[at], load_sem.at[half]).wait()
        pltpu.make_async_copy(kbuf.at[at], kbuf.at[at], load_sem.at[2 + half]).wait()

    weights = ((uq_ref, uq), (ur_ref, ur), (tab_ref, tab), (ab_ref, ab), (ve_ref, ve))

    def weight_copy(n):
        return pltpu.make_async_copy(weights[n][0], weights[n][1], load_sem.at[4 + n])

    weight_copy(0).start()
    load_units(range(BLOCK), 0)
    for n in range(1, 5):
        weight_copy(n).start()
    load_units(range(BLOCK, UNITS), 1)

    barrier = pltpu.get_barrier_semaphore()

    def greet(step, carry):
        pl.semaphore_signal(
            barrier,
            inc=1,
            device_id={"dp": me_dp, "tensor": lax.rem(me_t + step, RANKS)},
            device_id_type=MESH,
        )
        return carry

    lax.fori_loop(1, RANKS, greet, 0)
    for step in range(1, Y_DEV):
        pl.semaphore_signal(
            barrier, inc=1, device_id={"dp": y_peer(step), "tensor": me_t}, device_id_type=MESH
        )
    for step in range(1, X_DEV):
        pl.semaphore_signal(
            barrier, inc=1, device_id={"dp": x_peer(step), "tensor": me_t}, device_id_type=MESH
        )

    scale = (NOPE + ROPE) ** -0.5
    perm_row = lax.broadcasted_iota(jnp.int32, (PAIR, PAIR), 0)
    perm_col = lax.broadcasted_iota(jnp.int32, (PAIR, PAIR), 1)
    perm = (perm_col == (perm_row % MB) * DOC + perm_row // MB).astype(jnp.float32).astype(BF16)
    row_at = lax.broadcasted_iota(jnp.int32, (2 * PAIR, PAIR), 0) % PAIR
    row_micro = row_at % MB
    row_pos = row_at // MB
    key_at = lax.broadcasted_iota(jnp.int32, (2 * PAIR, PAIR), 1)
    key_pos = key_at % DOC
    causal = (key_at // DOC == row_micro) & (key_pos <= row_pos)
    diagonal = key_pos == row_pos
    out_at = lax.broadcasted_iota(jnp.int32, (PAIR, V_HEAD), 0)
    lane = lax.broadcasted_iota(jnp.int32, (PAIR, 128), 1)
    head_lane = [(lane // ROPE == h).astype(jnp.float32).astype(BF16) for h in range(2)]

    def compute(block):
        rows = slice(block * BLOCK * PAIR, (block + 1) * BLOCK * PAIR)
        x = xbuf[rows, :]
        nope = dot(x, uq[...]).astype(BF16)
        rope = dot(x, ur[...])
        mixed_all = [[], []]
        ordered = []
        for i in range(BLOCK):
            at = slice(i * PAIR, (i + 1) * PAIR)
            turned = rotate_pairs(rope[at], tab[0], tab[1]).astype(BF16)
            both = jnp.concatenate([nope[at], turned], 1)
            ordered.append(dot(perm, both).astype(BF16))
        ordered = jnp.concatenate(ordered, 0)
        absorbed = [
            dot(ordered[:, h * NOPE : (h + 1) * NOPE], ab[h * NOPE : (h + 1) * NOPE, :]).astype(BF16)
            for h in range(2)
        ]
        lengths = []
        for i in range(BLOCK):
            unit = block * BLOCK + i
            j, s = unit_place(unit)
            at = slice(i * PAIR, (i + 1) * PAIR)
            here = slice(unit * PAIR, (unit + 1) * PAIR)
            latent = kbuf[here, 0:KV_RANK]
            kr = kbuf[here, KV_RANK : KV_RANK + ROPE].astype(jnp.float32)
            kr = rotate_pairs(jnp.concatenate([kr, kr], 1), tab[0], tab[1]).astype(BF16)
            keys = jnp.concatenate([latent, kr], 1)
            qr = ordered[at, 2 * NOPE :]
            queries = jnp.concatenate(
                [
                    jnp.concatenate([absorbed[h][at], qr * head_lane[h]], 1)
                    for h in range(2)
                ],
                0,
            )
            scores = dot(queries, keys, ((1,), (1,)))
            slot = (me_dp * GROUP_DEV + j) * SLOTS + s
            pair_len = [len_ref[m, slot] for m in range(MB)]
            lengths.append(pair_len)
            live = jnp.where(row_micro == 0, pair_len[0], pair_len[1])
            allowed = causal & ((key_pos < live) | diagonal)
            scores = jnp.where(allowed, scores * scale, -jnp.inf)
            weight = jnp.exp(scores - jnp.max(scores, 1, keepdims=True))
            prob = (weight / jnp.sum(weight, 1, keepdims=True)).astype(BF16)
            mixed = dot(prob, latent).astype(BF16)
            for h in range(2):
                mixed_all[h].append(mixed[h * PAIR : (h + 1) * PAIR])
        for h in range(2):
            res = dot(jnp.concatenate(mixed_all[h], 0), ve[:, h * V_HEAD : (h + 1) * V_HEAD])
            for i in range(BLOCK):
                j, s = unit_place(block * BLOCK + i)
                live = jnp.where(out_at % MB == 0, lengths[i][0], lengths[i][1])
                part = jnp.where(out_at // MB < live, res[i * PAIR : (i + 1) * PAIR], 0.0)
                part = part.astype(BF16)
                if block == 0:
                    docs[j, h] = part
                else:
                    front.at[j, h].reshape((SLOTS - 1) * PAIR, V_HEAD)[
                        s * PAIR : (s + 1) * PAIR, :
                    ] = part

    weight_copy(0).wait()
    weight_copy(1).wait()
    weight_copy(2).wait()
    weight_copy(3).wait()
    weight_copy(4).wait()
    wait_units(0, BLOCK, 0)
    compute(0)

    pl.semaphore_wait(barrier, RANKS - 1 + X_DEV - 1 + Y_DEV - 1)

    def rows_of(c):
        return pl.ds(c * CHUNK, CHUNK)

    def y_copy(step, c):
        return pltpu.make_async_remote_copy(
            src_ref=docs.at[:, :, rows_of(c)],
            dst_ref=recv1[c].at[pl.ds(me_y * GROUP_DEV, GROUP_DEV)],
            send_sem=y_send.at[c, step - 1],
            recv_sem=y_recv.at[c, step - 1],
            device_id={"dp": y_peer(step), "tensor": me_t},
            device_id_type=MESH,
        )

    def relay(c):
        step, back = (1, 3) if c % 2 == 0 else (3, 1)
        slots = pl.ds(lax.rem(me_y + back, Y_DEV) * GROUP_DEV, GROUP_DEV)
        return pltpu.make_async_remote_copy(
            src_ref=recv1[c].at[slots],
            dst_ref=recv1[c].at[slots],
            send_sem=y_send.at[c, 1],
            recv_sem=y_recv.at[c, 1],
            device_id={"dp": y_peer(step), "tensor": me_t},
            device_id_type=MESH,
        )

    def pass_on(c):
        y_copy(1 if c % 2 == 0 else 3, c).wait_recv()
        relay(c).start()

    for step, c in ((1, 0), (3, 1), (1, 2), (3, 3), (1, 1), (3, 0), (1, 3), (3, 2)):
        y_copy(step, c).start()

    def own_copy(c):
        return pltpu.make_async_copy(
            docs.at[:, :, rows_of(c)],
            recv1[c].at[pl.ds(me_y * GROUP_DEV, GROUP_DEV)],
            own_sem.at[c],
        )

    for c in range(CHUNKS):
        own_copy(c).start()

    wait_units(BLOCK, UNITS - BLOCK, 1)
    compute(1)
    pass_on(0)
    pass_on(1)
    compute(2)
    pass_on(2)
    pass_on(3)

    mine = pl.ds(me_t * 2, 2)

    def to_rank(rank, source, target, send, recv):
        return pltpu.make_async_remote_copy(
            src_ref=source,
            dst_ref=target,
            send_sem=send.at[rank],
            recv_sem=recv.at[me_t],
            device_id={"dp": me_dp, "tensor": rank},
            device_id_type=MESH,
        )

    def whole(rank, source):
        return to_rank(rank, source, out_ref.at[mine], t_send, t_recv)

    def head_part(rank, source):
        return to_rank(rank, source, out_ref.at[mine, pl.ds(0, HALF)], h_send, h_recv)

    def tail_part(rank, source):
        return to_rank(
            rank, source, out_ref.at[mine, pl.ds(HALF, OWN_ROWS - HALF)], t_send, t_recv
        )

    def front_rows(rank):
        return front.at[rank // SHARE, :, pl.ds(lax.rem(rank, SHARE) * OWN_ROWS, OWN_ROWS)]

    def front_end(rank):
        return front.at[rank // SHARE, :, pl.ds(TAIL, HALF)]

    def final_rows(rank):
        start = (lax.rem(rank, SHARE) - CUT) * OWN_ROWS - HALF
        return final.at[rank // SHARE, :, pl.ds(start, OWN_ROWS)]

    def final_start(rank):
        return final.at[rank // SHARE, :, pl.ds(0, OWN_ROWS - HALF)]

    def send_front(step, carry):
        offset = RANKS // 2 + (1 - 2 * (step % 2)) * (step // 2)
        rank = lax.rem(me_t + offset, RANKS)
        place = lax.rem(rank, SHARE)

        @pl.when(place < CUT)
        def _():
            whole(rank, front_rows(rank)).start()

        @pl.when(place == CUT)
        def _():
            head_part(rank, front_end(rank)).start()

        return carry

    lax.fori_loop(1, RANKS, send_front, 0)
    my_place = lax.rem(me_t, SHARE)

    @pl.when(my_place < CUT)
    def _():
        pltpu.make_async_copy(front_rows(me_t), out_ref.at[mine], local_sem.at[1]).start()

    @pl.when(my_place == CUT)
    def _():
        pltpu.make_async_copy(
            front_end(me_t), out_ref.at[mine, pl.ds(0, HALF)], local_sem.at[2]
        ).start()

    even = lax.broadcasted_iota(jnp.int32, (CHUNK, V_HEAD), 0) % MB == 0

    def build(c):
        at = slice(c * CHUNK, (c + 1) * CHUNK)
        for step in range(X_DEV):
            x_at = lax.rem(me_x + step, X_DEV)
            for j in range(GROUP_DEV):
                group = (me_y * X_DEV + x_at) * GROUP_DEV + j
                index = []
                for m in range(MB):
                    mate = partner_ref[m, group]
                    index.append(mate // (X_DEV * GROUP_DEV) * GROUP_DEV + mate % GROUP_DEV)
                for h in range(2):
                    picked = jnp.where(
                        even, recv1[c][index[0], h], recv1[c][index[1], h]
                    )
                    if step == 0:
                        recv2[c][me_x, j, h] = picked
                    else:
                        snd2[step - 1, j, h, at, :] = picked

    def x_copy(step, c):
        return pltpu.make_async_remote_copy(
            src_ref=snd2.at[step - 1, :, :, rows_of(c)],
            dst_ref=recv2[c].at[me_x],
            send_sem=x_send.at[c, step - 1],
            recv_sem=x_recv.at[c, step - 1],
            device_id={"dp": x_peer(step), "tensor": me_t},
            device_id_type=MESH,
        )

    def first_half(c):
        own_copy(c).wait()
        y_copy(3 if c % 2 == 0 else 1, c).wait_recv()
        relay(c).wait_recv()
        build(c)
        for step in (2, 1, 3):
            x_copy(step, c).start()

    def second_half(c):
        for step in range(1, X_DEV):
            x_copy(step, c).wait_recv()
        at = slice(c * CHUNK // MB, (c + 1) * CHUNK // MB)
        for j in range(GROUP_DEV):
            group = me_dp * GROUP_DEV + j
            source = []
            light = []
            for m in range(MB):
                source.append((partner_ref[m, group] // GROUP_DEV) % X_DEV)
                live = jnp.int32(0)
                for s in range(SLOTS):
                    live += (len_ref[m, group * SLOTS + s] > 0).astype(jnp.int32)
                light.append(live < SLOTS)
            for h in range(2):
                picks = [
                    jnp.where(light[m], recv2[c][source[m], j, h], jnp.zeros((), BF16))
                    for m in range(MB)
                ]
                value = jnp.where(even, picks[0], picks[1])
                final[j, h, at] = value.reshape(CHUNK // MB, MB, V_HEAD)
        for place in PLACES[c]:

            def send_final(step, carry, place=place):
                rank = lax.rem(me_t // SHARE + 1 + step, GROUP_DEV) * SHARE + place

                @pl.when(rank != me_t)
                def _():
                    if place == CUT:
                        tail_part(rank, final_start(rank)).start()
                    else:
                        whole(rank, final_rows(rank)).start()

                return carry

            lax.fori_loop(0, GROUP_DEV, send_final, 0)

    first_half(0)
    first_half(1)
    second_half(0)
    first_half(2)
    second_half(1)
    first_half(3)
    second_half(2)
    second_half(3)

    @pl.when(my_place == CUT)
    def _():
        pltpu.make_async_copy(
            final_start(me_t), out_ref.at[mine, pl.ds(HALF, OWN_ROWS - HALF)], local_sem.at[1]
        ).start()

    @pl.when(my_place > CUT)
    def _():
        pltpu.make_async_copy(final_rows(me_t), out_ref.at[mine], local_sem.at[1]).start()

    def await_recv(step, carry):
        source = lax.rem(me_t + step, RANKS)
        theirs = pl.ds(source * 2, 2)

        def arrived(rows, recv):
            part = out_ref.at[theirs, rows]
            pltpu.make_async_copy(part, part, recv.at[source]).wait()

        @pl.when(my_place == CUT)
        def _():
            arrived(pl.ds(0, HALF), h_recv)
            arrived(pl.ds(HALF, OWN_ROWS - HALF), t_recv)

        @pl.when(my_place != CUT)
        def _():
            arrived(pl.ds(0, OWN_ROWS), t_recv)

        return carry

    def await_send(step, carry):
        rank = lax.rem(me_t + step, RANKS)
        place = lax.rem(rank, SHARE)

        @pl.when(place == CUT)
        def _():
            head_part(rank, front_end(rank)).wait_send()
            tail_part(rank, final_start(rank)).wait_send()

        @pl.when(place != CUT)
        def _():
            whole(rank, front.at[0, :, pl.ds(0, OWN_ROWS)]).wait_send()

        return carry

    lax.fori_loop(1, RANKS, await_send, 0)
    for c in range(CHUNKS):
        for step in (1, 3):
            y_copy(step, c).wait_send()
        relay(c).wait_send()
        for step in range(1, X_DEV):
            x_copy(step, c).wait_send()

    @pl.when(my_place == CUT)
    def _():
        pltpu.make_async_copy(
            front_end(me_t), out_ref.at[mine, pl.ds(0, HALF)], local_sem.at[2]
        ).wait()
        pltpu.make_async_copy(
            final_start(me_t), out_ref.at[mine, pl.ds(HALF, OWN_ROWS - HALF)], local_sem.at[1]
        ).wait()

    @pl.when(my_place != CUT)
    def _():
        pltpu.make_async_copy(
            front.at[0, :, pl.ds(0, OWN_ROWS)], out_ref.at[mine], local_sem.at[1]
        ).wait()

    lax.fori_loop(1, RANKS, await_recv, 0)


def attend(
    partner, doc_length, query, key, up_query, up_rope, key_absorb, value_expand
):
    smem = pl.BlockSpec(memory_space=pltpu.SMEM)
    anyw = pl.BlockSpec(memory_space=pl.ANY)
    part = (GROUP_DEV, 2, PAIR, V_HEAD)
    return pl.pallas_call(
        kernel,
        out_shape=jax.ShapeDtypeStruct((RANKS * 2, OWN_ROWS, MB, V_HEAD), BF16),
        in_specs=[smem, smem] + [anyw] * 7,
        out_specs=anyw,
        scratch_shapes=[
            pltpu.VMEM((UNITS * PAIR, Q_RANK), BF16),
            pltpu.VMEM((UNITS * PAIR, KV_RANK + ROPE), BF16),
            pltpu.VMEM((Q_RANK, 2 * NOPE), BF16),
            pltpu.VMEM((Q_RANK, 2 * ROPE), BF16),
            pltpu.VMEM((2 * NOPE, KV_RANK), BF16),
            pltpu.VMEM((KV_RANK, 2 * V_HEAD), BF16),
            pltpu.VMEM((2, PAIR, 128), jnp.float32),
            pltpu.VMEM((GROUP_DEV, 2, (SLOTS - 1) * DOC, MB, V_HEAD), BF16),
            pltpu.VMEM(part, BF16),
            *[pltpu.VMEM((Y_DEV * GROUP_DEV, 2, CHUNK, V_HEAD), BF16)] * CHUNKS,
            pltpu.VMEM((X_DEV - 1,) + part, BF16),
            *[pltpu.VMEM((X_DEV, GROUP_DEV, 2, CHUNK, V_HEAD), BF16)] * CHUNKS,
            pltpu.VMEM((GROUP_DEV, 2, DOC, MB, V_HEAD), BF16),
            pltpu.SemaphoreType.DMA((9,)),
            pltpu.SemaphoreType.DMA((3,)),
            pltpu.SemaphoreType.DMA((CHUNKS,)),
            pltpu.SemaphoreType.DMA((CHUNKS, Y_DEV - 1)),
            pltpu.SemaphoreType.DMA((CHUNKS, Y_DEV - 1)),
            pltpu.SemaphoreType.DMA((CHUNKS, X_DEV - 1)),
            pltpu.SemaphoreType.DMA((CHUNKS, X_DEV - 1)),
            pltpu.SemaphoreType.DMA((RANKS,)),
            pltpu.SemaphoreType.DMA((RANKS,)),
            pltpu.SemaphoreType.DMA((RANKS,)),
            pltpu.SemaphoreType.DMA((RANKS,)),
        ],
        compiler_params=pltpu.CompilerParams(collective_id=0, has_side_effects=True),
        name="attend",
    )(
        partner,
        doc_length,
        query,
        key,
        up_query,
        up_rope,
        key_absorb,
        value_expand,
        jnp.asarray(rope_tables()),
    )


def body(
    query_latent, key_latent, partner, doc_length, up_query, up_rope, key_absorb, value_expand
):
    result = attend(
        partner,
        doc_length,
        query_latent,
        key_latent,
        up_query,
        up_rope,
        key_absorb,
        value_expand,
    )
    return result.transpose(2, 1, 0, 3).reshape(MB, OWN_ROWS, RANKS * 2 * V_HEAD)


def solution(mesh):
    in_specs = (
        P(None, "dp", None),
        P(None, "dp", None),
        P(),
        P(),
        P(None, "tensor"),
        P(None, "tensor"),
        P("tensor", None),
        P(None, "tensor"),
    )
    out_specs = P(None, ("dp", "tensor"), None)
    return jax.shard_map(body, mesh=mesh, in_specs=in_specs, out_specs=out_specs, check_vma=False)
```
